32 devices in a mesh: groups: 2 (over y), weight: 4 (over z), token: 2 (over x), sub: 2 (over core).
Axes of the slice: x: 2, y: 2, z: 4, core: 2. Of those that a mesh axis runs over, the one named last changes fastest.
Arguments:
- tokens: bfloat16 [512, 8192], P(('groups', 'token'), ('weight', 'sub')), parts along dimension 0, may hold values from -6 to 6
- gate_blocks: bfloat16 [2, 8, 384, 128, 128], P('token', ('weight', 'sub')), may hold values from -0.09375 to 0.09375
- up_blocks: bfloat16 [2, 8, 384, 128, 128], P('token', ('weight', 'sub')), may hold values from -0.09375 to 0.09375
- gate_list: int32 [2, 8, 384], P(None, ('weight', 'sub')), may hold values from 0 to 511, as said below
- gate_count: int32 [2, 8], P(None, ('weight', 'sub')), may hold values from 128 to 384, as said below
- up_list: int32 [2, 8, 384], P(None, ('weight', 'sub')), may hold values from 0 to 511, as said below
- up_count: int32 [2, 8], P(None, ('weight', 'sub')), may hold values from 128 to 384, as said below
- cotangent: bfloat16 [512, 16384], P(('groups', 'token'), ('weight', 'sub')), parts along dimension 0, may hold values from -0.375 to 0.375
Outputs:
- hidden: bfloat16 [512, 16384], P(('groups', 'token'), ('weight', 'sub')), parts along dimension 0
- gate_grad: bfloat16 [4, 8, 384, 128, 128], P(('groups', 'token'), ('weight', 'sub')), parts along dimension 0
- up_grad: bfloat16 [4, 8, 384, 128, 128], P(('groups', 'token'), ('weight', 'sub')), parts along dimension 0
The draws below stay inside these ranges and needn't reach their ends.
There are 2 independent parts, one for each index of `groups`. The reference program is written for one: setup_inputs(seed, part) draws one part's arguments, and reference() takes and returns one part's arrays. A program takes and returns all parts, laid end to end along the dimension named above; an argument that names none is the same for every part. Nothing has to cross between parts.
Inputs may be any that keep to these rules, and one draw needn't show every extreme that they name: `gate_list`: the 384 entries of one owner are distinct block positions. `up_list`: the 384 entries of one owner are distinct block positions. The first gate_count[t, c] slots of owner (t, c) are live; some owner has exactly 384. The first up_count[t, c] slots of owner (t, c) are live; some owner has exactly 384.
All inputs are finite; a program needn't handle non-finite values.
Results may differ from the reference program's by a relative error of at most 0.0059.
Values may be sent and summed in bfloat16 or wider, within the bound.
A program may use at most 448 MiB of HBM per device.

```python
import jax
import jax.numpy as jnp
from jax import lax

D = 8192
FF = 16384
BLK = 128
TOKENS = 256
PANELS = 8
BPOS = 512
CAP = 384
N_TOKEN = 2


def list_draw(base_key):
    owner_keys = jax.random.split(base_key, N_TOKEN * PANELS)

    def one_owner(owner_key):
        return jax.random.permutation(owner_key, BPOS)[:CAP]
    permuted = jax.vmap(one_owner)(owner_keys)
    return permuted.astype(jnp.int32).reshape(N_TOKEN, PANELS, CAP)


def count_draw(base_key):
    counted = jax.random.randint(base_key, (N_TOKEN * PANELS,), BPOS - CAP, CAP + 1, dtype=jnp.int32)
    chosen = jax.random.randint(jax.random.fold_in(base_key, 7), (), 0, N_TOKEN * PANELS, dtype=jnp.int32)
    flattened = jnp.where(jnp.arange(N_TOKEN * PANELS, dtype=jnp.int32) == chosen, CAP, counted)
    return flattened.astype(jnp.int32).reshape(N_TOKEN, PANELS)


def draw_gate_list(key, part):
    return list_draw(jax.random.fold_in(key, 11))


def draw_up_list(key, part):
    return list_draw(jax.random.fold_in(key, 12))


def draw_gate_count(key, part):
    return count_draw(jax.random.fold_in(key, 21))


def draw_up_count(key, part):
    return count_draw(jax.random.fold_in(key, 22))


def level_of(key, dims, cuts, least, high):
    gain, own = 1.0, jax.random.fold_in(key, 6)
    for position, parts in cuts:
        draws = jnp.exp(jax.random.uniform(jax.random.fold_in(own, position), (parts,), jnp.float32, least / len(cuts), high / len(cuts)))
        gain = gain * jnp.repeat(draws, dims[position] // parts).reshape([-1 if axis == position else 1 for axis in range(len(dims))])
    return gain


def bell_draw(stream_key, extent, spread, bound, cuts=(), held_as=jnp.bfloat16):
    result = jax.random.normal(stream_key, extent, jnp.float32) * spread
    if len(cuts) > 0:
        result = level_of(stream_key, extent, cuts, -0.22, 0.18) * result
    return jnp.clip(result, min=-bound, max=bound).astype(held_as)


def setup_inputs(seed: int = 0, part: int = 0) -> dict:
    arg_keys = jax.random.split(jax.random.key(seed), 9)
    part_keys = jax.random.split(jax.random.fold_in(arg_keys[8], part), 9)
    tokens = bell_draw(part_keys[0], (TOKENS, D), 1.0, 6.0, ((0, 2), (1, 8)))
    gate_blocks = bell_draw(arg_keys[1], (N_TOKEN, PANELS, CAP, BLK, BLK), (D // 2) ** -0.5, 0.09375, ((0, 2), (1, 8)))
    up_blocks = bell_draw(arg_keys[2], (N_TOKEN, PANELS, CAP, BLK, BLK), (D // 2) ** -0.5, 0.09375, ((0, 2), (1, 8)))
    gate_list = draw_gate_list(jax.random.fold_in(arg_keys[8], 71), part)
    gate_count = draw_gate_count(jax.random.fold_in(arg_keys[8], 71), part)
    up_list = draw_up_list(jax.random.fold_in(arg_keys[8], 71), part)
    up_count = draw_up_count(jax.random.fold_in(arg_keys[8], 71), part)
    cotangent = bell_draw(part_keys[7], (TOKENS, FF), (TOKENS ** -0.5), 0.375, ((0, 2), (1, 8)))
    return {"tokens": tokens, "gate_blocks": gate_blocks, "up_blocks": up_blocks, "gate_list": gate_list, "gate_count": gate_count, "up_list": up_list, "up_count": up_count, "cotangent": cotangent}


def expand(blocks, slot_lists, slot_counts):
    n_owner_rows, n_panels, capacity = slot_lists.shape
    row_blocks = D // BLK // n_owner_rows
    col_blocks = FF // BLK // n_panels
    live_slots = jnp.arange(capacity, dtype=jnp.int32)[None, None, :] < slot_counts[:, :, None]
    kept_blocks = jnp.where(live_slots[..., None, None], blocks, jnp.zeros_like(blocks))
    dense_matrix = jnp.zeros((n_owner_rows, n_panels, row_blocks * col_blocks, BLK, BLK), blocks.dtype)
    owner_rows = jnp.arange(n_owner_rows, dtype=jnp.int32)[:, None, None]
    owner_cols = jnp.arange(n_panels, dtype=jnp.int32)[None, :, None]
    dense_matrix = dense_matrix.at[owner_rows, owner_cols, slot_lists].set(kept_blocks)
    dense_matrix = dense_matrix.reshape(n_owner_rows, n_panels, row_blocks, col_blocks, BLK, BLK)
    return dense_matrix.transpose(0, 2, 4, 1, 3, 5).reshape(D, FF)

def block_grad(tokens, delta, slot_lists, slot_counts):
    n_owner_rows, n_panels, capacity = slot_lists.shape
    row_blocks = D // BLK // n_owner_rows
    col_blocks = FF // BLK // n_panels
    group_rows = tokens.reshape(n_owner_rows, -1, D)
    group_deltas = delta.reshape(n_owner_rows, -1, FF)

    def add_group(running, group_pair):
        group_term = jnp.dot(group_pair[0].T, group_pair[1], preferred_element_type=jnp.float32)
        group_term = lax.optimization_barrier(group_term.astype(jnp.bfloat16))
        return (running + group_term.astype(jnp.float32), None)
    running, _ = lax.scan(add_group, jnp.zeros((D, FF), jnp.float32), (group_rows, group_deltas))
    arranged = running.reshape(n_owner_rows, row_blocks, BLK, n_panels, col_blocks, BLK)
    arranged = arranged.transpose(0, 3, 1, 4, 2, 5).reshape(n_owner_rows, n_panels, row_blocks * col_blocks, BLK, BLK)
    selected = jnp.take_along_axis(arranged, slot_lists[:, :, :, None, None], axis=2)
    live_slots = jnp.arange(capacity, dtype=jnp.int32)[None, None, :] < slot_counts[:, :, None]
    return jnp.where(live_slots[..., None, None], selected, jnp.zeros_like(selected)).astype(jnp.bfloat16)

def reference(tokens, gate_blocks, up_blocks, gate_list, gate_count, up_list, up_count, cotangent):
    gate_weight = expand(gate_blocks, gate_list, gate_count)
    up_weight = expand(up_blocks, up_list, up_count)
    gate_sum = jnp.dot(tokens, gate_weight, preferred_element_type=jnp.float32)
    up_sum = jnp.dot(tokens, up_weight, preferred_element_type=jnp.float32)
    sigmoid_gate = jax.nn.sigmoid(gate_sum)
    silu_gate = gate_sum * sigmoid_gate
    hidden = (silu_gate * up_sum).astype(jnp.bfloat16)
    cot_values = cotangent.astype(jnp.float32)
    gate_delta = (cot_values * up_sum * sigmoid_gate * (1.0 + gate_sum * (1.0 - sigmoid_gate))).astype(jnp.bfloat16)
    up_delta = (cot_values * silu_gate).astype(jnp.bfloat16)
    gate_grad = block_grad(tokens, gate_delta, gate_list, gate_count)
    up_grad = block_grad(tokens, up_delta, up_list, up_count)
    return (hidden, gate_grad, up_grad)
```

```python
import jax
import jax.numpy as jnp
from jax import lax
from jax.experimental import pallas as pl
from jax.experimental.pallas import tpu as pltpu
from jax.sharding import PartitionSpec as P

MESH = pl.DeviceIdType.MESH
LANES = 128


def up_to(size, step):
    return -(-size // step) * step


def fill_table(table, lists, counts, me, capacity, positions):
    n = up_to(positions, LANES) // LANES
    table[...] = jnp.zeros(table.shape, jnp.int32)
    slot = lax.broadcasted_iota(jnp.int32, (LANES, LANES), 0)
    lane = lax.broadcasted_iota(jnp.int32, (LANES, LANES), 1)
    for m in range(2):
        count = counts[m][me]
        found = [jnp.full((1, LANES), capacity, jnp.int32) for _ in range(n)]
        for g in range(lists.shape[3] // LANES):
            row = lists[m, me, :, g * LANES : (g + 1) * LANES]
            column = jnp.broadcast_to(row, (LANES, LANES)).T
            column = jnp.where(slot + g * LANES < count, column, -1)
            for i in range(n):
                hit = jnp.where(column == lane + i * LANES, slot + g * LANES, capacity)
                found[i] = jnp.minimum(found[i], jnp.min(hit, axis=0, keepdims=True))
        for i in range(n):
            table[m * n + i : m * n + i + 1, :] = found[i]
        table[2 * n + m : 2 * n + m + 1, :] = jnp.full((1, LANES), count, jnp.int32)


def exchange_kernel(
    tokens, gate_blocks, up_blocks, gate_list, up_list, gate_count, up_count, cotangent,
    hidden, turned, delta, table,
    held_gate, held_up, lists, slots, slots_s, own_x, other_x, flipped, own, sent, landed, delta_all, hidden_all, cot_all,
    block_sems, list_sems, table_sems, cot_sem, mine_sem,
    z_send, z_recv, x_send, x_recv, s_send, s_recv, p_send, p_recv, d_send, d_recv, out_sems, delta_sems,
):
    held = (held_gate, held_up)
    owners = lax.axis_size("token")
    line = lax.axis_size("weight")
    subs = lax.axis_size("sub")
    me = lax.axis_index("token")
    here = lax.axis_index("weight")
    sub = lax.axis_index("sub")
    capacity, block, _ = gate_blocks.shape
    rows, local = tokens.shape
    depth = own_x.shape[2]
    width = hidden.shape[1]
    cols = width // block
    panels = line // owners
    parts = z_recv.shape[1]
    part = rows // parts
    chunks = p_send.shape[2]
    piece = width // chunks
    tile = min(piece, 256)
    tables = up_to(depth * width // block**2, LANES) // LANES
    sibling = {"sub": 1 - sub}
    ahead = [{"token": lax.rem(me + d, owners)} for d in range(owners)]
    behind = [{"token": lax.rem(me + owners - d, owners)} for d in range(owners)]
    left, right = {"weight": here - 1}, {"weight": here + 1}
    inner = here > 0
    outer = here < line - 1

    barrier = pltpu.get_barrier_semaphore()

    @pl.when(inner)
    def _():
        pl.semaphore_signal(barrier, inc=1, device_id=left, device_id_type=MESH)

    @pl.when(outer)
    def _():
        pl.semaphore_signal(barrier, inc=1, device_id=right, device_id_type=MESH)

    for d in range(1, owners):
        pl.semaphore_signal(barrier, inc=1, device_id=ahead[d], device_id_type=MESH)
    pl.semaphore_signal(barrier, inc=1, device_id=sibling, device_id_type=MESH)

    def span(q):
        return pl.ds(pl.multiple_of(q * part, part), part)

    def panel(o):
        return pl.ds(pl.multiple_of((lax.rem(o, panels) * subs + sub) * local, local), local)

    def own_at(o, q):
        return own_x.at[lax.div(o, panels), span(q), panel(o)]

    mine = pltpu.make_async_copy(tokens, own_x.at[lax.div(here, panels), :, panel(here)], mine_sem)
    list_copies = [
        pltpu.make_async_copy(source, lists.at[m], list_sems.at[m])
        for m, source in enumerate((gate_list, up_list))
    ]
    block_copies = [
        pltpu.make_async_copy(source, held[m].at[pl.ds(0, capacity)], block_sems.at[m])
        for m, source in enumerate((gate_blocks, up_blocks))
    ]
    cot_copy = pltpu.make_async_copy(cotangent, cot_all, cot_sem)
    mine.start()
    for copy in list_copies:
        copy.start()
    block_copies[0].start()

    def z_copy(source, o, q, side):
        return pltpu.make_async_remote_copy(
            src_ref=source, dst_ref=own_at(o, q), send_sem=z_send.at[side, o, q], recv_sem=z_recv.at[o, q],
            device_id=(left, right)[side], device_id_type=MESH,
        )

    def cross_copy(source, o, q):
        half = lax.div(o, panels)
        d = lax.rem(half + owners - me, owners)
        return pltpu.make_async_remote_copy(
            src_ref=source, dst_ref=other_x.at[d - 1, span(q), panel(o)],
            send_sem=x_send.at[o, q], recv_sem=x_recv.at[d - 1, lax.rem(o, panels), q],
            device_id={"token": half}, device_id_type=MESH,
        )

    def sibling_copy(source, target, d, o, q):
        j = lax.rem(o, panels)
        return pltpu.make_async_remote_copy(
            src_ref=source, dst_ref=target, send_sem=s_send.at[d, j, q], recv_sem=s_recv.at[d, j, q],
            device_id=sibling, device_id_type=MESH,
        )

    def hand_on(source, o, q):
        @pl.when(lax.div(o, panels) == me)
        def _():
            sibling_copy(source, own_at(o, q), 0, o, q).start()

        @pl.when(lax.div(o, panels) != me)
        def _():
            cross_copy(source, o, q).start()

    pl.semaphore_wait(
        barrier, owners + inner.astype(jnp.int32) + outer.astype(jnp.int32)
    )
    for q in range(parts):
        source = tokens.at[q * part : (q + 1) * part, :]

        @pl.when(inner)
        def _():
            z_copy(source, here, q, 0).start()

        @pl.when(outer)
        def _():
            z_copy(source, here, q, 1).start()

        hand_on(source, here, q)
    block_copies[1].start()
    cot_copy.start()

    zero = jnp.zeros((block, block), held_gate.dtype)
    for m in range(2):
        held[m][capacity] = zero
    for copy in list_copies:
        copy.wait()
    fill_table(slots, lists, (gate_count, up_count), me, capacity, depth * width // block**2)
    table_copies = [
        pltpu.make_async_copy(slots, slots_s, table_sems.at[0]),
        pltpu.make_async_copy(slots, table, table_sems.at[1]),
    ]
    for copy in table_copies:
        copy.start()

    def take_over(k):
        for d in range(1, owners):

            @pl.loop(0, panels)
            def _(j):
                o = me * panels + j

                @pl.when(lax.abs(o - here) == k)
                def _():
                    for q in range(parts):
                        there = other_x.at[d - 1, span(q), panel(o)]
                        pltpu.make_async_remote_copy(
                            src_ref=there, dst_ref=there, send_sem=s_send.at[d, j, q],
                            recv_sem=x_recv.at[d - 1, j, q], device_id=sibling, device_id_type=MESH,
                        ).wait_recv()
                        sibling_copy(there, there, d, o, q).start()

    @pl.loop(1, line)
    def _(k):
        for side in range(2):
            o = here + k if side == 0 else here - k

            @pl.when((o >= 0) & (o < line))
            def _():
                for q in range(parts):
                    z_copy(own_at(o, q), o, q, side).wait_recv()

                    @pl.when((inner, outer)[side])
                    def _():
                        z_copy(own_at(o, q), o, q, side).start()

                    hand_on(own_at(o, q), o, q)

        take_over(k - 1)

    take_over(line - 1)

    def sibling_wait(d, recv):
        @pl.loop(0, panels)
        def _(j):
            o = me * panels + j
            for q in range(parts):
                there = own_at(o, q) if d == 0 else other_x.at[d - 1, span(q), panel(o)]
                copy = sibling_copy(there, there, d, o, q)
                if recv:
                    copy.wait_recv()
                else:
                    copy.wait_send()

    def part_copy(d, m, c):
        at = pl.ds(pl.multiple_of(c * piece, piece), piece)
        return pltpu.make_async_remote_copy(
            src_ref=sent.at[d - 1, m, :, at], dst_ref=landed.at[d - 1, m, :, at],
            send_sem=p_send.at[d - 1, m, c], recv_sem=p_recv.at[d - 1, m, c],
            device_id=behind[d], device_id_type=MESH,
        )

    def delta_copy(d, m, c):
        at = pl.ds(pl.multiple_of(c * piece, piece), piece)
        return pltpu.make_async_remote_copy(
            src_ref=delta_all.at[m, pl.ds(0, rows), at], dst_ref=delta_all.at[m, pl.ds(d * rows, rows), at],
            send_sem=d_send.at[d - 1, m, c], recv_sem=d_recv.at[d - 1, m, c],
            device_id=ahead[d], device_id_type=MESH,
        )

    def delta_out(m, c):
        at = pl.ds(pl.multiple_of(c * piece, piece), piece)
        return pltpu.make_async_copy(delta_all.at[m, :, at], delta.at[m, :, at], delta_sems.at[m, c])

    def product(x, m, first):
        strips = []
        for r in range(depth // block):
            line_of = []
            for q in range(tile // block):
                at = first + q + (r * cols) % LANES
                line_of.append(held[m][slots_s[m * tables + (r * cols) // LANES, at]])
            strips.append(jnp.concatenate(line_of, axis=1))
        return jnp.dot(x, jnp.concatenate(strips, axis=0), preferred_element_type=jnp.float32)

    def pass_on(m):
        for d in range(1, owners):

            @pl.loop(0, chunks)
            def _(c):
                for i in range(piece // tile):
                    at = pl.ds(pl.multiple_of(c * piece + i * tile, tile), tile)
                    first = c * (piece // block) + i * (tile // block)
                    sent[d - 1, m, :, at] = product(other_x[d - 1], m, first).astype(sent.dtype)
                part_copy(d, m, c).start()

    def keep(m):
        @pl.loop(0, width // tile)
        def _(c):
            at = pl.ds(pl.multiple_of(c * tile, tile), tile)
            own[m, :, at] = product(own_x[me], m, c * (tile // block))

    def total(m, c):
        for d in range(1, owners):
            part_copy(d, m, c).wait_recv()
        at = pl.ds(pl.multiple_of(c * piece, piece), piece)
        value = own[m, :, at]
        for d in range(1, owners):
            value = value + landed[d - 1, m, :, at].astype(jnp.float32)
        return value

    table_copies[0].wait()
    block_copies[0].wait()
    for d in range(1, owners):
        sibling_wait(d, True)
    pass_on(0)
    mine.wait()
    sibling_wait(0, True)
    keep(0)
    block_copies[1].wait()
    pass_on(1)
    keep(1)
    cot_copy.wait()

    @pl.loop(0, chunks)
    def _(c):
        at = pl.ds(pl.multiple_of(c * piece, piece), piece)
        gate = total(0, c)
        own[0, :, at] = gate
        silu = gate * jax.nn.sigmoid(gate)
        delta_all[1, 0:rows, at] = (cot_all[:, at].astype(jnp.float32) * silu).astype(delta_all.dtype)
        for d in range(1, owners):
            delta_copy(d, 1, c).start()

    flip = min(depth, 256)
    for d in range(owners):

        @pl.loop(0, depth // flip)
        def _(i):
            at = pl.ds(pl.multiple_of(i * flip, flip), flip)
            value = own_x[me, :, at] if d == 0 else other_x[d - 1, :, at]
            flipped[at, d * rows : (d + 1) * rows] = value.T

    turned_out = pltpu.make_async_copy(flipped, turned, out_sems.at[0])
    turned_out.start()

    @pl.loop(0, chunks)
    def _(c):
        at = pl.ds(pl.multiple_of(c * piece, piece), piece)
        up = total(1, c)
        gate = own[0, :, at]
        sigmoid = jax.nn.sigmoid(gate)
        hidden_all[:, at] = (gate * sigmoid * up).astype(hidden_all.dtype)
        slope = sigmoid * (1.0 + gate * (1.0 - sigmoid))
        value = cot_all[:, at].astype(jnp.float32) * up * slope
        delta_all[0, 0:rows, at] = value.astype(delta_all.dtype)
        for d in range(1, owners):
            delta_copy(d, 0, c).start()

    hidden_out = pltpu.make_async_copy(hidden_all, hidden, out_sems.at[1])
    hidden_out.start()

    for m in (1, 0):

        @pl.loop(0, chunks)
        def _(c):
            for d in range(1, owners):
                delta_copy(d, m, c).wait_recv()
            delta_out(m, c).start()

    for q in range(parts):

        @pl.loop(0, line)
        def _(o):
            @pl.when(inner & (o >= here))
            def _():
                z_copy(own_at(o, q), o, q, 0).wait_send()

            @pl.when(outer & (o <= here))
            def _():
                z_copy(own_at(o, q), o, q, 1).wait_send()

            @pl.when(lax.div(o, panels) != me)
            def _():
                cross_copy(own_at(o, q), o, q).wait_send()

    for d in range(owners):
        sibling_wait(d, False)
    for m in range(2):

        @pl.loop(0, chunks)
        def _(c):
            for d in range(1, owners):
                part_copy(d, m, c).wait_send()
                delta_copy(d, m, c).wait_send()
            delta_out(m, c).wait()

    table_copies[1].wait()
    turned_out.wait()
    hidden_out.wait()


def exchange(tokens, gate_blocks, up_blocks, lists, counts, cotangent, owners, line, subs):
    rows, local = tokens.shape
    capacity, block, _ = gate_blocks.shape
    width = cotangent.shape[1]
    depth = local * line * subs // owners
    piece = min(width, 256)
    chunks = width // piece
    panels = line // owners
    parts = 4 if rows % 64 == 0 else 1
    everyone = owners * rows
    table_rows = up_to(2 * up_to(depth * width // block**2, LANES) // LANES + 2, 8)
    dma = pltpu.SemaphoreType.DMA
    hbm = pl.BlockSpec(memory_space=pl.ANY)
    smem = pl.BlockSpec(memory_space=pltpu.SMEM)
    bf16 = jnp.bfloat16
    return pl.pallas_call(
        exchange_kernel,
        out_shape=(
            jax.ShapeDtypeStruct((rows, width), bf16),
            jax.ShapeDtypeStruct((depth, everyone), bf16),
            jax.ShapeDtypeStruct((2, everyone, width), bf16),
            jax.ShapeDtypeStruct((table_rows, LANES), jnp.int32),
        ),
        in_specs=[hbm] * 5 + [smem] * 2 + [hbm],
        out_specs=(hbm,) * 4,
        scratch_shapes=[
            pltpu.VMEM((capacity + 1, block, block), bf16),
            pltpu.VMEM((capacity + 1, block, block), bf16),
            pltpu.VMEM((2, *lists[0].shape), jnp.int32),
            pltpu.VMEM((table_rows, LANES), jnp.int32),
            pltpu.SMEM((table_rows, LANES), jnp.int32),
            pltpu.VMEM((owners, rows, depth), bf16),
            pltpu.VMEM((owners - 1, rows, depth), bf16),
            pltpu.VMEM((depth, everyone), bf16),
            pltpu.VMEM((2, rows, width), jnp.float32),
            pltpu.VMEM((owners - 1, 2, rows, width), bf16),
            pltpu.VMEM((owners - 1, 2, rows, width), bf16),
            pltpu.VMEM((2, everyone, width), bf16),
            pltpu.VMEM((rows, width), bf16),
            pltpu.VMEM((rows, width), bf16),
            dma((2,)),
            dma((2,)),
            dma((2,)),
            dma,
            dma,
            dma((2, line, parts)),
            dma((line, parts)),
            dma((line, parts)),
            dma((owners - 1, panels, parts)),
            dma((owners, panels, parts)),
            dma((owners, panels, parts)),
            dma((owners - 1, 2, chunks)),
            dma((owners - 1, 2, chunks)),
            dma((owners - 1, 2, chunks)),
            dma((owners - 1, 2, chunks)),
            dma((2,)),
            dma((2, chunks)),
        ],
        compiler_params=pltpu.CompilerParams(
            collective_id=0, has_side_effects=True, vmem_limit_bytes=56 << 20
        ),
        cost_estimate=pl.CostEstimate(
            flops=4 * everyone * depth * width,
            bytes_accessed=4 * capacity * block**2,
            transcendentals=2 * rows * width,
        ),
    )(tokens, gate_blocks, up_blocks, *lists, *counts, cotangent)


def grad_kernel(table, turned, delta, kept, hidden, gate_grad, up_grad, dense, zero, sems, hidden_sem):
    capacity, block, _ = gate_grad.shape
    depth = turned.shape[0]
    width = delta.shape[2]
    cols = width // block
    tables = up_to(dense.shape[1], LANES) // LANES
    strip = min(depth, 2048)
    tile = min(width, 512)
    outs = (gate_grad, up_grad)
    hidden_copy = pltpu.make_async_copy(kept, hidden, hidden_sem)
    hidden_copy.start()
    zero[...] = jnp.zeros(zero.shape, zero.dtype)
    for m in range(2):

        @pl.loop(table[2 * tables + m, 0], capacity)
        def _(k):
            pltpu.make_async_copy(zero, outs[m].at[k], sems.at[m]).start()

    for m in range(2):

        @pl.loop(0, width // tile)
        def _(c):
            at = pl.ds(pl.multiple_of(c * tile, tile), tile)

            @pl.loop(0, depth // strip)
            def _(i):
                rows = pl.ds(pl.multiple_of(i * strip, strip), strip)
                term = jnp.dot(
                    turned[rows, :], delta[m, :, at], preferred_element_type=jnp.float32
                ).astype(dense.dtype)
                spots = [
                    (r, q, (i * (strip // block) + r) * cols + c * (tile // block) + q)
                    for r in range(strip // block)
                    for q in range(tile // block)
                ]
                for r, q, p in spots:
                    dense[m, p] = term[r * block : (r + 1) * block, q * block : (q + 1) * block]
                for r, q, p in spots:
                    slot = table[m * tables + p // LANES, p % LANES]

                    @pl.when(slot < capacity)
                    def _():
                        pltpu.make_async_copy(dense.at[m, p], outs[m].at[slot], sems.at[m]).start()

    for m in range(2):
        pltpu.make_async_copy(outs[m], outs[m], sems.at[m]).wait()
    hidden_copy.wait()


def block_grads(table, turned, delta, hidden, capacity, block):
    depth = turned.shape[0]
    width = delta.shape[2]
    shape = jax.ShapeDtypeStruct((capacity, block, block), jnp.bfloat16)
    hbm = pl.BlockSpec(memory_space=pl.ANY)
    vmem = pl.BlockSpec(memory_space=pltpu.VMEM)
    return pl.pallas_call(
        grad_kernel,
        out_shape=(jax.ShapeDtypeStruct(hidden.shape, hidden.dtype), shape, shape),
        in_specs=[pl.BlockSpec(memory_space=pltpu.SMEM), vmem, vmem, hbm],
        out_specs=(hbm,) * 3,
        scratch_shapes=[
            pltpu.VMEM((2, depth * width // block**2, block, block), jnp.bfloat16),
            pltpu.VMEM((block, block), jnp.bfloat16),
            pltpu.SemaphoreType.DMA((2,)),
            pltpu.SemaphoreType.DMA,
        ],
        compiler_params=pltpu.CompilerParams(vmem_limit_bytes=56 << 20),
        cost_estimate=pl.CostEstimate(
            flops=4 * depth * width * turned.shape[1],
            bytes_accessed=4 * capacity * block * block,
            transcendentals=0,
        ),
    )(table, turned, delta, hidden)


def shards(tokens, gate_blocks, up_blocks, gate_list, gate_count, up_list, up_count, cotangent):
    owners = lax.axis_size("token")
    capacity, block = gate_blocks.shape[2:4]
    short = up_to(capacity, LANES) - capacity
    lists = [gate_list, up_list]
    if short:
        lists = [jnp.pad(x, ((0, 0), (0, 0), (0, short)), constant_values=-1) for x in lists]
    counts = [gate_count.reshape(owners), up_count.reshape(owners)]
    hidden, turned, delta, table = exchange(
        tokens, gate_blocks[0, 0], up_blocks[0, 0], lists, counts, cotangent,
        owners, lax.axis_size("weight"), lax.axis_size("sub"),
    )
    hidden, gate_grad, up_grad = block_grads(table, turned, delta, hidden, capacity, block)
    shape = (1, 1, capacity, block, block)
    return (hidden, gate_grad.reshape(shape), up_grad.reshape(shape))


def solution(mesh):
    return jax.shard_map(
        shards,
        mesh=mesh,
        in_specs=(
            P(("groups", "token"), ("weight", "sub")),
            P("token", ("weight", "sub"), None, None, None),
            P("token", ("weight", "sub"), None, None, None),
            P(None, ("weight", "sub"), None),
            P(None, ("weight", "sub")),
            P(None, ("weight", "sub"), None),
            P(None, ("weight", "sub")),
            P(("groups", "token"), ("weight", "sub")),
        ),
        out_specs=(
            P(("groups", "token"), ("weight", "sub")),
            P(("groups", "token"), ("weight", "sub"), None, None, None),
            P(("groups", "token"), ("weight", "sub"), None, None, None),
        ),
        check_vma=False,
    )
```

```python
import jax
import jax.numpy as jnp
from jax import lax
from jax.experimental import pallas as pl
from jax.experimental.pallas import tpu as pltpu
from jax.sharding import PartitionSpec as P

MESH = pl.DeviceIdType.MESH
LANES = 128


def up_to(size, step):
    return -(-size // step) * step


def fill_table(table, lists, counts, me, positions):
    n = up_to(positions, LANES) // LANES
    groups = lists.shape[3] // LANES
    table[...] = jnp.zeros(table.shape, jnp.int32)
    slot = lax.broadcasted_iota(jnp.int32, (LANES, LANES), 0)
    lane = lax.broadcasted_iota(jnp.int32, (LANES, LANES), 1)
    for m in range(2):
        count = counts[m][me]
        found = [jnp.full((1, LANES), positions, jnp.int32) for _ in range(n)]
        for g in range(groups):
            row = lists[m, me, :, g * LANES : (g + 1) * LANES]
            column = jnp.broadcast_to(row, (LANES, LANES)).T
            column = jnp.where(slot + g * LANES < count, column, -1)
            for i in range(n):
                hit = jnp.where(column == lane + i * LANES, slot + g * LANES, positions)
                found[i] = jnp.minimum(found[i], jnp.min(hit, axis=0, keepdims=True))
            at = 2 * n + m * groups + g
            live = lane[0:1] + g * LANES < count
            table[at : at + 1, :] = jnp.where(live, row, positions)
        for i in range(n):
            table[m * n + i : m * n + i + 1, :] = found[i]


def exchange_kernel(
    tokens, gate_blocks, up_blocks, gate_list, up_list, gate_count, up_count, cotangent,
    hidden, terms_gate, terms_up, table,
    lists, slots, slots_s, own_x, other_x, flipped, own, sent, landed, delta_all, cot_all,
    block_sems, list_sems, table_sems, cot_sem, mine_sem,
    z_send, z_recv, x_send, x_recv, s_send, s_recv, p_send, p_recv, d_send, d_recv,
):
    held = (terms_gate, terms_up)
    owners = lax.axis_size("token")
    line = lax.axis_size("weight")
    subs = lax.axis_size("sub")
    me = lax.axis_index("token")
    here = lax.axis_index("weight")
    sub = lax.axis_index("sub")
    capacity, block, _ = gate_blocks.shape
    rows, local = tokens.shape
    depth = own_x.shape[2]
    width = hidden.shape[1]
    cols = width // block
    panels = line // owners
    parts = z_recv.shape[1]
    part = rows // parts
    chunks = p_send.shape[2]
    piece = width // chunks
    tile = min(piece, 256)
    positions = depth * width // block**2
    tables = up_to(positions, LANES) // LANES
    sibling = {"sub": 1 - sub}
    ahead = [{"token": lax.rem(me + d, owners)} for d in range(owners)]
    behind = [{"token": lax.rem(me + owners - d, owners)} for d in range(owners)]
    left, right = {"weight": here - 1}, {"weight": here + 1}
    inner = here > 0
    outer = here < line - 1

    barrier = pltpu.get_barrier_semaphore()

    @pl.when(inner)
    def _():
        pl.semaphore_signal(barrier, inc=1, device_id=left, device_id_type=MESH)

    @pl.when(outer)
    def _():
        pl.semaphore_signal(barrier, inc=1, device_id=right, device_id_type=MESH)

    for d in range(1, owners):
        pl.semaphore_signal(barrier, inc=1, device_id=ahead[d], device_id_type=MESH)
    pl.semaphore_signal(barrier, inc=1, device_id=sibling, device_id_type=MESH)

    def span(q):
        return pl.ds(pl.multiple_of(q * part, part), part)

    def panel(o):
        return pl.ds(pl.multiple_of((lax.rem(o, panels) * subs + sub) * local, local), local)

    def own_at(o, q):
        return own_x.at[lax.div(o, panels), span(q), panel(o)]

    mine = pltpu.make_async_copy(tokens, own_x.at[lax.div(here, panels), :, panel(here)], mine_sem)
    list_copies = [
        pltpu.make_async_copy(source, lists.at[m], list_sems.at[m])
        for m, source in enumerate((gate_list, up_list))
    ]
    block_copies = [
        pltpu.make_async_copy(source, held[m].at[pl.ds(0, capacity)], block_sems.at[m])
        for m, source in enumerate((gate_blocks, up_blocks))
    ]
    cot_copy = pltpu.make_async_copy(cotangent, cot_all, cot_sem)
    mine.start()
    for copy in list_copies:
        copy.start()
    block_copies[0].start()

    def z_copy(source, o, q, side):
        return pltpu.make_async_remote_copy(
            src_ref=source, dst_ref=own_at(o, q), send_sem=z_send.at[side, o, q], recv_sem=z_recv.at[o, q],
            device_id=(left, right)[side], device_id_type=MESH,
        )

    def cross_copy(source, o, q):
        half = lax.div(o, panels)
        d = lax.rem(half + owners - me, owners)
        return pltpu.make_async_remote_copy(
            src_ref=source, dst_ref=other_x.at[d - 1, span(q), panel(o)],
            send_sem=x_send.at[o, q], recv_sem=x_recv.at[d - 1, lax.rem(o, panels), q],
            device_id={"token": half}, device_id_type=MESH,
        )

    def sibling_copy(source, target, d, o, q):
        j = lax.rem(o, panels)
        return pltpu.make_async_remote_copy(
            src_ref=source, dst_ref=target, send_sem=s_send.at[d, j, q], recv_sem=s_recv.at[d, j, q],
            device_id=sibling, device_id_type=MESH,
        )

    def hand_on(source, o, q):
        @pl.when(lax.div(o, panels) == me)
        def _():
            sibling_copy(source, own_at(o, q), 0, o, q).start()

        @pl.when(lax.div(o, panels) != me)
        def _():
            cross_copy(source, o, q).start()

    pl.semaphore_wait(
        barrier, owners + inner.astype(jnp.int32) + outer.astype(jnp.int32)
    )
    def send_mine(q, side):
        @pl.when((inner, outer)[side])
        def _():
            z_copy(tokens.at[q * part : (q + 1) * part, :], here, q, side).start()

    at_home = lax.div(here, panels) == me
    gives_way = (at_home & (me < owners - 1), at_home & (me > 0))
    first = parts // 2 if line <= 4 else parts
    for q in range(parts):
        for side in range(2):
            if q < first:
                send_mine(q, side)
            else:

                @pl.when(jnp.logical_not(gives_way[side]))
                def _():
                    send_mine(q, side)

        hand_on(tokens.at[q * part : (q + 1) * part, :], here, q)
    block_copies[1].start()
    cot_copy.start()

    zero = jnp.zeros((block, block), terms_gate.dtype)
    for m in range(2):
        held[m][positions] = zero
    for copy in list_copies:
        copy.wait()
    fill_table(slots, lists, (gate_count, up_count), me, positions)
    table_copies = [
        pltpu.make_async_copy(slots, slots_s, table_sems.at[0]),
        pltpu.make_async_copy(slots, table, table_sems.at[1]),
    ]
    for copy in table_copies:
        copy.start()

    def take_over(k):
        for d in range(1, owners):

            @pl.loop(0, panels)
            def _(j):
                o = me * panels + j

                @pl.when(lax.abs(o - here) == k)
                def _():
                    for q in range(parts):
                        there = other_x.at[d - 1, span(q), panel(o)]
                        pltpu.make_async_remote_copy(
                            src_ref=there, dst_ref=there, send_sem=s_send.at[d, j, q],
                            recv_sem=x_recv.at[d - 1, j, q], device_id=sibling, device_id_type=MESH,
                        ).wait_recv()
                        sibling_copy(there, there, d, o, q).start()

    @pl.loop(1, line)
    def _(k):
        for side in range(2):
            o = here + k if side == 0 else here - k

            goes_on = (inner, outer)[side]

            @pl.when((o >= 0) & (o < line) & (goes_on | (lax.div(o, panels) != me)))
            def _():
                for q in range(parts):
                    z_copy(own_at(o, q), o, q, side).wait_recv()

                    @pl.when(goes_on)
                    def _():
                        z_copy(own_at(o, q), o, q, side).start()

                    hand_on(own_at(o, q), o, q)

            @pl.when(gives_way[side] & (k == (line - 1 - here if side == 0 else here)))
            def _():
                for q in range(first, parts):
                    send_mine(q, side)

        take_over(k - 1)

    take_over(line - 1)

    def take_late():
        @pl.loop(0, panels)
        def _(j):
            o = me * panels + j

            @pl.when((jnp.logical_not(inner) & (o > here)) | (jnp.logical_not(outer) & (o < here)))
            def _():
                for q in range(parts):
                    z_copy(own_at(o, q), o, q, 0).wait_recv()
                    sibling_copy(own_at(o, q), own_at(o, q), 0, o, q).start()

    def sibling_wait(d, recv):
        @pl.loop(0, panels)
        def _(j):
            o = me * panels + j
            for q in range(parts):
                there = own_at(o, q) if d == 0 else other_x.at[d - 1, span(q), panel(o)]
                copy = sibling_copy(there, there, d, o, q)
                if recv:
                    copy.wait_recv()
                else:
                    copy.wait_send()

    def part_copy(d, m, c):
        at = pl.ds(pl.multiple_of(c * piece, piece), piece)
        return pltpu.make_async_remote_copy(
            src_ref=sent.at[d - 1, m, :, at], dst_ref=landed.at[d - 1, m, :, at],
            send_sem=p_send.at[d - 1, m, c], recv_sem=p_recv.at[d - 1, m, c],
            device_id=behind[d], device_id_type=MESH,
        )

    def delta_copy(d, m, c):
        at = pl.ds(pl.multiple_of(c * piece, piece), piece)
        return pltpu.make_async_remote_copy(
            src_ref=delta_all.at[m, pl.ds(0, rows), at], dst_ref=delta_all.at[m, pl.ds(d * rows, rows), at],
            send_sem=d_send.at[d - 1, m, c], recv_sem=d_recv.at[d - 1, m, c],
            device_id=ahead[d], device_id_type=MESH,
        )

    def product(x, m, first):
        strips = []
        for r in range(depth // block):
            line_of = []
            for q in range(tile // block):
                at = first + q + (r * cols) % LANES
                line_of.append(held[m][slots_s[m * tables + (r * cols) // LANES, at]])
            strips.append(jnp.concatenate(line_of, axis=1))
        return jnp.dot(x, jnp.concatenate(strips, axis=0), preferred_element_type=jnp.float32)

    def pass_on(m):
        for d in range(1, owners):

            @pl.loop(0, chunks)
            def _(c):
                for i in range(piece // tile):
                    at = pl.ds(pl.multiple_of(c * piece + i * tile, tile), tile)
                    first = c * (piece // block) + i * (tile // block)
                    sent[d - 1, m, :, at] = product(other_x[d - 1], m, first).astype(sent.dtype)
                part_copy(d, m, c).start()

    def keep(m):
        @pl.loop(0, width // tile)
        def _(c):
            at = pl.ds(pl.multiple_of(c * tile, tile), tile)
            own[m, :, at] = product(own_x[me], m, c * (tile // block))

    def total(m, c):
        for d in range(1, owners):
            part_copy(d, m, c).wait_recv()
        at = pl.ds(pl.multiple_of(c * piece, piece), piece)
        value = own[m, :, at]
        for d in range(1, owners):
            value = value + landed[d - 1, m, :, at].astype(jnp.float32)
        return value

    table_copies[0].wait()
    block_copies[0].wait()
    for d in range(1, owners):
        sibling_wait(d, True)
    pass_on(0)
    mine.wait()
    take_late()
    sibling_wait(0, True)
    keep(0)
    block_copies[1].wait()
    pass_on(1)
    keep(1)
    cot_copy.wait()

    @pl.loop(0, chunks)
    def _(c):
        at = pl.ds(pl.multiple_of(c * piece, piece), piece)
        gate = total(0, c)
        own[0, :, at] = gate
        silu = gate * jax.nn.sigmoid(gate)
        delta_all[1, 0:rows, at] = (cot_all[:, at].astype(jnp.float32) * silu).astype(delta_all.dtype)
        for d in range(1, owners):
            delta_copy(d, 1, c).start()

    flip = min(depth, 256)
    for d in range(owners):

        @pl.loop(0, depth // flip)
        def _(i):
            at = pl.ds(pl.multiple_of(i * flip, flip), flip)
            value = own_x[me, :, at] if d == 0 else other_x[d - 1, :, at]
            flipped[at, d * rows : (d + 1) * rows] = value.T

    @pl.loop(0, chunks)
    def _(c):
        at = pl.ds(pl.multiple_of(c * piece, piece), piece)
        up = total(1, c)
        gate = own[0, :, at]
        sigmoid = jax.nn.sigmoid(gate)
        hidden[:, at] = (gate * sigmoid * up).astype(hidden.dtype)
        slope = sigmoid * (1.0 + gate * (1.0 - sigmoid))
        value = cot_all[:, at].astype(jnp.float32) * up * slope
        delta_all[0, 0:rows, at] = value.astype(delta_all.dtype)
        for d in range(1, owners):
            delta_copy(d, 0, c).start()

    for m in (1, 0):

        @pl.loop(0, chunks)
        def _(c):
            for d in range(1, owners):
                delta_copy(d, m, c).wait_recv()
            at = pl.ds(pl.multiple_of(c * piece, piece), piece)
            term = jnp.dot(
                flipped[...], delta_all[m, :, at], preferred_element_type=jnp.float32
            ).astype(terms_gate.dtype)
            for r in range(depth // block):
                for q in range(piece // block):
                    p = r * cols + c * (piece // block) + q
                    held[m][p] = term[r * block : (r + 1) * block, q * block : (q + 1) * block]

    for q in range(parts):

        @pl.loop(0, line)
        def _(o):
            @pl.when(inner & (o >= here))
            def _():
                z_copy(own_at(o, q), o, q, 0).wait_send()

            @pl.when(outer & (o <= here))
            def _():
                z_copy(own_at(o, q), o, q, 1).wait_send()

            @pl.when(lax.div(o, panels) != me)
            def _():
                cross_copy(own_at(o, q), o, q).wait_send()

    for d in range(owners):
        sibling_wait(d, False)
    for m in range(2):

        @pl.loop(0, chunks)
        def _(c):
            for d in range(1, owners):
                part_copy(d, m, c).wait_send()
                delta_copy(d, m, c).wait_send()

    table_copies[1].wait()


def exchange(tokens, gate_blocks, up_blocks, lists, counts, cotangent, owners, line, subs):
    rows, local = tokens.shape
    capacity, block, _ = gate_blocks.shape
    width = cotangent.shape[1]
    depth = local * line * subs // owners
    piece = min(width, 256)
    chunks = width // piece
    panels = line // owners
    parts = 4 if rows % 64 == 0 else 1
    everyone = owners * rows
    positions = depth * width // block**2
    table_rows = up_to(2 * up_to(positions, LANES) // LANES + 2 * lists[0].shape[2] // LANES, 8)
    blocks = pltpu.VMEM((positions + 1, block, block), jnp.bfloat16)
    dma = pltpu.SemaphoreType.DMA
    hbm = pl.BlockSpec(memory_space=pl.ANY)
    smem = pl.BlockSpec(memory_space=pltpu.SMEM)
    vmem = pl.BlockSpec(memory_space=pltpu.VMEM)
    bf16 = jnp.bfloat16
    return pl.pallas_call(
        exchange_kernel,
        out_shape=(
            pltpu.VMEM((rows, width), bf16),
            blocks,
            blocks,
            jax.ShapeDtypeStruct((table_rows, LANES), jnp.int32),
        ),
        in_specs=[hbm] * 5 + [smem] * 2 + [hbm],
        out_specs=(vmem, vmem, vmem, hbm),
        scratch_shapes=[
            pltpu.VMEM((2, *lists[0].shape), jnp.int32),
            pltpu.VMEM((table_rows, LANES), jnp.int32),
            pltpu.SMEM((table_rows, LANES), jnp.int32),
            pltpu.VMEM((owners, rows, depth), bf16),
            pltpu.VMEM((owners - 1, rows, depth), bf16),
            pltpu.VMEM((depth, everyone), bf16),
            pltpu.VMEM((2, rows, width), jnp.float32),
            pltpu.VMEM((owners - 1, 2, rows, width), bf16),
            pltpu.VMEM((owners - 1, 2, rows, width), bf16),
            pltpu.VMEM((2, everyone, width), bf16),
            pltpu.VMEM((rows, width), bf16),
            dma((2,)),
            dma((2,)),
            dma((2,)),
            dma,
            dma,
            dma((2, line, parts)),
            dma((line, parts)),
            dma((line, parts)),
            dma((owners - 1, panels, parts)),
            dma((owners, panels, parts)),
            dma((owners, panels, parts)),
            dma((owners - 1, 2, chunks)),
            dma((owners - 1, 2, chunks)),
            dma((owners - 1, 2, chunks)),
            dma((owners - 1, 2, chunks)),
        ],
        compiler_params=pltpu.CompilerParams(
            collective_id=0, has_side_effects=True, vmem_limit_bytes=28 << 20
        ),
        cost_estimate=pl.CostEstimate(
            flops=4 * everyone * depth * width,
            bytes_accessed=4 * capacity * block**2,
            transcendentals=2 * rows * width,
        ),
    )(tokens, gate_blocks, up_blocks, *lists, *counts, cotangent)


def place_kernel(table, terms_gate, terms_up, kept, hidden, gate_grad, up_grad, sems, hidden_sem):
    capacity = gate_grad.shape[0]
    positions = terms_gate.shape[0] - 1
    groups = up_to(capacity, LANES) // LANES
    base = 2 * up_to(positions, LANES) // LANES
    hidden_copy = pltpu.make_async_copy(kept, hidden, hidden_sem)
    hidden_copy.start()
    pairs = ((terms_gate, gate_grad), (terms_up, up_grad))
    for m, (terms, out) in enumerate(pairs):
        for g in range(groups):

            @pl.loop(0, min(LANES, capacity - g * LANES), unroll=8)
            def _(j):
                source = terms.at[table[base + m * groups + g, j]]
                pltpu.make_async_copy(source, out.at[g * LANES + j], sems.at[m]).start()

    for m, (_, out) in enumerate(pairs):
        pltpu.make_async_copy(out, out, sems.at[m]).wait()
    hidden_copy.wait()


def place(table, terms_gate, terms_up, hidden, capacity):
    shape = jax.ShapeDtypeStruct((capacity, *terms_gate.shape[1:]), jnp.bfloat16)
    hbm = pl.BlockSpec(memory_space=pl.ANY)
    vmem = pl.BlockSpec(memory_space=pltpu.VMEM)
    return pl.pallas_call(
        place_kernel,
        out_shape=(jax.ShapeDtypeStruct(hidden.shape, hidden.dtype), shape, shape),
        in_specs=[pl.BlockSpec(memory_space=pltpu.SMEM), vmem, vmem, vmem],
        out_specs=(hbm,) * 3,
        scratch_shapes=[pltpu.SemaphoreType.DMA((2,)), pltpu.SemaphoreType.DMA],
        compiler_params=pltpu.CompilerParams(vmem_limit_bytes=28 << 20),
        cost_estimate=pl.CostEstimate(
            flops=0, bytes_accessed=4 * capacity * terms_gate.shape[1] ** 2, transcendentals=0
        ),
    )(
        table,
        pltpu.with_memory_space_constraint(terms_gate, pltpu.VMEM),
        pltpu.with_memory_space_constraint(terms_up, pltpu.VMEM),
        pltpu.with_memory_space_constraint(hidden, pltpu.VMEM),
    )


def shards(tokens, gate_blocks, up_blocks, gate_list, gate_count, up_list, up_count, cotangent):
    owners = lax.axis_size("token")
    capacity, block = gate_blocks.shape[2:4]
    short = up_to(capacity, LANES) - capacity
    lists = [gate_list, up_list]
    if short:
        lists = [jnp.pad(x, ((0, 0), (0, 0), (0, short)), constant_values=-1) for x in lists]
    counts = [gate_count.reshape(owners), up_count.reshape(owners)]
    hidden, terms_gate, terms_up, table = exchange(
        tokens, gate_blocks[0, 0], up_blocks[0, 0], lists, counts, cotangent,
        owners, lax.axis_size("weight"), lax.axis_size("sub"),
    )
    hidden, gate_grad, up_grad = place(table, terms_gate, terms_up, hidden, capacity)
    shape = (1, 1, capacity, block, block)
    return (hidden, gate_grad.reshape(shape), up_grad.reshape(shape))


def solution(mesh):
    return jax.shard_map(
        shards,
        mesh=mesh,
        in_specs=(
            P(("groups", "token"), ("weight", "sub")),
            P("token", ("weight", "sub"), None, None, None),
            P("token", ("weight", "sub"), None, None, None),
            P(None, ("weight", "sub"), None),
            P(None, ("weight", "sub")),
            P(None, ("weight", "sub"), None),
            P(None, ("weight", "sub")),
            P(("groups", "token"), ("weight", "sub")),
        ),
        out_specs=(
            P(("groups", "token"), ("weight", "sub")),
            P(("groups", "token"), ("weight", "sub"), None, None, None),
            P(("groups", "token"), ("weight", "sub"), None, None, None),
        ),
        check_vma=False,
    )
```

```python
import jax
import jax.numpy as jnp
from jax import lax
from jax.experimental import pallas as pl
from jax.experimental.pallas import tpu as pltpu
from jax.sharding import PartitionSpec as P

MESH = pl.DeviceIdType.MESH
LANES = 128


def up_to(size, step):
    return -(-size // step) * step


def fill_table(table, lists, counts, me, positions):
    n = up_to(positions, LANES) // LANES
    groups = lists.shape[3] // LANES
    table[...] = jnp.zeros(table.shape, jnp.int32)
    slot = lax.broadcasted_iota(jnp.int32, (LANES, LANES), 0)
    lane = lax.broadcasted_iota(jnp.int32, (LANES, LANES), 1)
    for m in range(2):
        count = counts[m][me]
        found = [jnp.full((1, LANES), positions, jnp.int32) for _ in range(n)]
        for g in range(groups):
            row = lists[m, me, :, g * LANES : (g + 1) * LANES]
            column = jnp.broadcast_to(row, (LANES, LANES)).T
            column = jnp.where(slot + g * LANES < count, column, -1)
            for i in range(n):
                hit = jnp.where(column == lane + i * LANES, slot + g * LANES, positions)
                found[i] = jnp.minimum(found[i], jnp.min(hit, axis=0, keepdims=True))
            at = 2 * n + m * groups + g
            live = lane[0:1] + g * LANES < count
            table[at : at + 1, :] = jnp.where(live, row, positions)
        for i in range(n):
            table[m * n + i : m * n + i + 1, :] = found[i]


def exchange_kernel(
    tokens, gate_blocks, up_blocks, gate_list, up_list, gate_count, up_count, cotangent,
    hidden, terms_gate, terms_up, table,
    lists, slots, slots_s, own_x, other_x, flipped, own, sent, landed, delta_all, cot_all,
    block_sems, list_sems, table_sems, cot_sem, mine_sem,
    z_send, z_recv, x_send, x_recv, s_send, s_recv, p_send, p_recv, d_send, d_recv,
):
    held = (terms_gate, terms_up)
    owners = lax.axis_size("token")
    line = lax.axis_size("weight")
    subs = lax.axis_size("sub")
    me = lax.axis_index("token")
    here = lax.axis_index("weight")
    sub = lax.axis_index("sub")
    capacity, block, _ = gate_blocks.shape
    rows, local = tokens.shape
    depth = own_x.shape[2]
    width = hidden.shape[1]
    cols = width // block
    panels = line // owners
    parts = z_recv.shape[1]
    part = rows // parts
    chunks = p_send.shape[2]
    halves = p_send.shape[1] - 1
    piece = width // chunks
    tile = min(piece, 256)
    positions = depth * width // block**2
    tables = up_to(positions, LANES) // LANES
    sibling = {"sub": 1 - sub}
    ahead = [{"token": lax.rem(me + d, owners)} for d in range(owners)]
    behind = [{"token": lax.rem(me + owners - d, owners)} for d in range(owners)]
    left, right = {"weight": here - 1}, {"weight": here + 1}
    inner = here > 0
    outer = here < line - 1

    barrier = pltpu.get_barrier_semaphore()

    @pl.when(inner)
    def _():
        pl.semaphore_signal(barrier, inc=1, device_id=left, device_id_type=MESH)

    @pl.when(outer)
    def _():
        pl.semaphore_signal(barrier, inc=1, device_id=right, device_id_type=MESH)

    for d in range(1, owners):
        pl.semaphore_signal(barrier, inc=1, device_id=ahead[d], device_id_type=MESH)
    pl.semaphore_signal(barrier, inc=1, device_id=sibling, device_id_type=MESH)

    def span(q):
        return pl.ds(pl.multiple_of(q * part, part), part)

    def panel(o):
        return pl.ds(pl.multiple_of((lax.rem(o, panels) * subs + sub) * local, local), local)

    def own_at(o, q):
        return own_x.at[lax.div(o, panels), span(q), panel(o)]

    mine = pltpu.make_async_copy(tokens, own_x.at[lax.div(here, panels), :, panel(here)], mine_sem)
    list_copies = [
        pltpu.make_async_copy(source, lists.at[m], list_sems.at[m])
        for m, source in enumerate((gate_list, up_list))
    ]
    block_copies = [
        pltpu.make_async_copy(source, held[m].at[pl.ds(0, capacity)], block_sems.at[m])
        for m, source in enumerate((gate_blocks, up_blocks))
    ]
    cot_copy = pltpu.make_async_copy(cotangent, cot_all, cot_sem)
    mine.start()
    for copy in list_copies:
        copy.start()

    def z_copy(source, o, q, side):
        return pltpu.make_async_remote_copy(
            src_ref=source, dst_ref=own_at(o, q), send_sem=z_send.at[side, o, q], recv_sem=z_recv.at[o, q],
            device_id=(left, right)[side], device_id_type=MESH,
        )

    def cross_copy(source, o, q):
        half = lax.div(o, panels)
        d = lax.rem(half + owners - me, owners)
        return pltpu.make_async_remote_copy(
            src_ref=source, dst_ref=other_x.at[d - 1, span(q), panel(o)],
            send_sem=x_send.at[o, q], recv_sem=x_recv.at[d - 1, lax.rem(o, panels), q],
            device_id={"token": half}, device_id_type=MESH,
        )

    def sibling_copy(source, target, d, o, q):
        j = lax.rem(o, panels)
        return pltpu.make_async_remote_copy(
            src_ref=source, dst_ref=target, send_sem=s_send.at[d, j, q], recv_sem=s_recv.at[d, j, q],
            device_id=sibling, device_id_type=MESH,
        )

    def hand_on(source, o, q):
        @pl.when(lax.div(o, panels) == me)
        def _():
            sibling_copy(source, own_at(o, q), 0, o, q).start()

        @pl.when(lax.div(o, panels) != me)
        def _():
            cross_copy(source, o, q).start()

    pl.semaphore_wait(
        barrier, owners + inner.astype(jnp.int32) + outer.astype(jnp.int32)
    )
    def send_mine(q, side):
        @pl.when((inner, outer)[side])
        def _():
            z_copy(tokens.at[q * part : (q + 1) * part, :], here, q, side).start()

    at_home = lax.div(here, panels) == me
    gives_way = (at_home & (me < owners - 1), at_home & (me > 0))
    first = parts // 2 if line <= 4 else parts
    for q in range(parts):
        for side in range(2):
            if q < first:
                send_mine(q, side)
            else:

                @pl.when(jnp.logical_not(gives_way[side]))
                def _():
                    send_mine(q, side)

        hand_on(tokens.at[q * part : (q + 1) * part, :], here, q)
    for copy in block_copies:
        copy.start()
    cot_copy.start()

    zero = jnp.zeros((block, block), terms_gate.dtype)
    for m in range(2):
        held[m][positions] = zero
    for copy in list_copies:
        copy.wait()
    fill_table(slots, lists, (gate_count, up_count), me, positions)
    table_copies = [
        pltpu.make_async_copy(slots, slots_s, table_sems.at[0]),
        pltpu.make_async_copy(slots, table, table_sems.at[1]),
    ]
    for copy in table_copies:
        copy.start()

    def take_over(k, pieces):
        for d in range(1, owners):

            @pl.loop(0, panels)
            def _(j):
                o = me * panels + j

                @pl.when(lax.abs(o - here) == k)
                def _():
                    for q in pieces:
                        there = other_x.at[d - 1, span(q), panel(o)]
                        pltpu.make_async_remote_copy(
                            src_ref=there, dst_ref=there, send_sem=s_send.at[d, j, q],
                            recv_sem=x_recv.at[d - 1, j, q], device_id=sibling, device_id_type=MESH,
                        ).wait_recv()
                        sibling_copy(there, there, d, o, q).start()

    @pl.loop(1, line)
    def _(k):
        for side in range(2):
            o = here + k if side == 0 else here - k

            goes_on = (inner, outer)[side]

            @pl.when((o >= 0) & (o < line) & (goes_on | (lax.div(o, panels) != me)))
            def _():
                for q in range(parts):
                    z_copy(own_at(o, q), o, q, side).wait_recv()

                    @pl.when(goes_on)
                    def _():
                        z_copy(own_at(o, q), o, q, side).start()

                    hand_on(own_at(o, q), o, q)

            @pl.when(gives_way[side] & (k == (line - 1 - here if side == 0 else here)))
            def _():
                for q in range(first, parts):
                    send_mine(q, side)

        take_over(k - 1, range(parts))

    def take_late():
        @pl.loop(0, panels)
        def _(j):
            o = me * panels + j

            @pl.when((jnp.logical_not(inner) & (o > here)) | (jnp.logical_not(outer) & (o < here)))
            def _():
                for q in range(parts):
                    z_copy(own_at(o, q), o, q, 0).wait_recv()
                    sibling_copy(own_at(o, q), own_at(o, q), 0, o, q).start()

    def sibling_wait(d, recv, pieces):
        @pl.loop(0, panels)
        def _(j):
            o = me * panels + j
            for q in pieces:
                there = own_at(o, q) if d == 0 else other_x.at[d - 1, span(q), panel(o)]
                copy = sibling_copy(there, there, d, o, q)
                if recv:
                    copy.wait_recv()
                else:
                    copy.wait_send()

    def part_copy(d, m, h, c):
        size = rows // halves if m == 0 else rows
        across = pl.ds(h * size, size)
        at = pl.ds(pl.multiple_of(c * piece, piece), piece)
        return pltpu.make_async_remote_copy(
            src_ref=sent.at[d - 1, m, across, at], dst_ref=landed.at[d - 1, m, across, at],
            send_sem=p_send.at[d - 1, m * halves + h, c], recv_sem=p_recv.at[d - 1, m * halves + h, c],
            device_id=behind[d], device_id_type=MESH,
        )

    def delta_copy(d, m, c):
        at = pl.ds(pl.multiple_of(c * piece, piece), piece)
        return pltpu.make_async_remote_copy(
            src_ref=delta_all.at[m, pl.ds(0, rows), at], dst_ref=delta_all.at[m, pl.ds(d * rows, rows), at],
            send_sem=d_send.at[d - 1, m, c], recv_sem=d_recv.at[d - 1, m, c],
            device_id=ahead[d], device_id_type=MESH,
        )

    def product(x, m, first):
        strips = []
        for r in range(depth // block):
            line_of = []
            for q in range(tile // block):
                at = first + q + (r * cols) % LANES
                line_of.append(held[m][slots_s[m * tables + (r * cols) // LANES, at]])
            strips.append(jnp.concatenate(line_of, axis=1))
        return jnp.dot(x, jnp.concatenate(strips, axis=0), preferred_element_type=jnp.float32)

    def pass_on(m, h, size):
        for d in range(1, owners):

            @pl.loop(0, chunks)
            def _(c):
                for i in range(piece // tile):
                    at = pl.ds(pl.multiple_of(c * piece + i * tile, tile), tile)
                    first = c * (piece // block) + i * (tile // block)
                    value = product(other_x[d - 1, h * size : (h + 1) * size, :], m, first)
                    sent[d - 1, m, h * size : (h + 1) * size, at] = value.astype(sent.dtype)
                part_copy(d, m, h, c).start()

    def keep(m):
        @pl.loop(0, width // tile)
        def _(c):
            at = pl.ds(pl.multiple_of(c * tile, tile), tile)
            own[m, :, at] = product(own_x[me], m, c * (tile // block))

    def total(m, c):
        for d in range(1, owners):
            for h in range(halves if m == 0 else 1):
                part_copy(d, m, h, c).wait_recv()
        at = pl.ds(pl.multiple_of(c * piece, piece), piece)
        value = own[m, :, at]
        for d in range(1, owners):
            value = value + landed[d - 1, m, :, at].astype(jnp.float32)
        return value

    table_copies[0].wait()
    block_copies[0].wait()
    for h in range(halves):
        pieces = range(h * parts // halves, (h + 1) * parts // halves)
        take_over(line - 1, pieces)
        for d in range(1, owners):
            sibling_wait(d, True, pieces)
        pass_on(0, h, rows // halves)
    block_copies[1].wait()
    pass_on(1, 0, rows)
    mine.wait()
    take_late()
    sibling_wait(0, True, range(parts))
    keep(0)
    cot_copy.wait()

    @pl.loop(0, chunks)
    def _(c):
        at = pl.ds(pl.multiple_of(c * piece, piece), piece)
        gate = total(0, c)
        own[0, :, at] = gate
        silu = gate * jax.nn.sigmoid(gate)
        delta_all[1, 0:rows, at] = (cot_all[:, at].astype(jnp.float32) * silu).astype(delta_all.dtype)
        for d in range(1, owners):
            delta_copy(d, 1, c).start()

    keep(1)

    flip = min(depth, 256)
    for d in range(owners):

        @pl.loop(0, depth // flip)
        def _(i):
            at = pl.ds(pl.multiple_of(i * flip, flip), flip)
            value = own_x[me, :, at] if d == 0 else other_x[d - 1, :, at]
            flipped[at, d * rows : (d + 1) * rows] = value.T

    @pl.loop(0, chunks)
    def _(c):
        at = pl.ds(pl.multiple_of(c * piece, piece), piece)
        up = total(1, c)
        gate = own[0, :, at]
        sigmoid = jax.nn.sigmoid(gate)
        hidden[:, at] = (gate * sigmoid * up).astype(hidden.dtype)
        slope = sigmoid * (1.0 + gate * (1.0 - sigmoid))
        value = cot_all[:, at].astype(jnp.float32) * up * slope
        delta_all[0, 0:rows, at] = value.astype(delta_all.dtype)
        for d in range(1, owners):
            delta_copy(d, 0, c).start()

    for m in (1, 0):

        @pl.loop(0, chunks)
        def _(c):
            for d in range(1, owners):
                delta_copy(d, m, c).wait_recv()
            at = pl.ds(pl.multiple_of(c * piece, piece), piece)
            term = jnp.dot(
                flipped[...], delta_all[m, :, at], preferred_element_type=jnp.float32
            ).astype(terms_gate.dtype)
            for r in range(depth // block):
                for q in range(piece // block):
                    p = r * cols + c * (piece // block) + q
                    held[m][p] = term[r * block : (r + 1) * block, q * block : (q + 1) * block]

    for q in range(parts):

        @pl.loop(0, line)
        def _(o):
            @pl.when(inner & (o >= here))
            def _():
                z_copy(own_at(o, q), o, q, 0).wait_send()

            @pl.when(outer & (o <= here))
            def _():
                z_copy(own_at(o, q), o, q, 1).wait_send()

            @pl.when(lax.div(o, panels) != me)
            def _():
                cross_copy(own_at(o, q), o, q).wait_send()

    for d in range(owners):
        sibling_wait(d, False, range(parts))
    for m in range(2):

        @pl.loop(0, chunks)
        def _(c):
            for d in range(1, owners):
                for h in range(halves if m == 0 else 1):
                    part_copy(d, m, h, c).wait_send()
                delta_copy(d, m, c).wait_send()

    table_copies[1].wait()


def exchange(tokens, gate_blocks, up_blocks, lists, counts, cotangent, owners, line, subs):
    rows, local = tokens.shape
    capacity, block, _ = gate_blocks.shape
    width = cotangent.shape[1]
    depth = local * line * subs // owners
    piece = min(width, 256)
    chunks = width // piece
    panels = line // owners
    parts = 4 if rows % 64 == 0 else 1
    halves = 2 if parts > 1 else 1
    everyone = owners * rows
    positions = depth * width // block**2
    table_rows = up_to(2 * up_to(positions, LANES) // LANES + 2 * lists[0].shape[2] // LANES, 8)
    blocks = pltpu.VMEM((positions + 1, block, block), jnp.bfloat16)
    dma = pltpu.SemaphoreType.DMA
    hbm = pl.BlockSpec(memory_space=pl.ANY)
    smem = pl.BlockSpec(memory_space=pltpu.SMEM)
    vmem = pl.BlockSpec(memory_space=pltpu.VMEM)
    bf16 = jnp.bfloat16
    return pl.pallas_call(
        exchange_kernel,
        out_shape=(
            pltpu.VMEM((rows, width), bf16),
            blocks,
            blocks,
            jax.ShapeDtypeStruct((table_rows, LANES), jnp.int32),
        ),
        in_specs=[hbm] * 5 + [smem] * 2 + [hbm],
        out_specs=(vmem, vmem, vmem, hbm),
        scratch_shapes=[
            pltpu.VMEM((2, *lists[0].shape), jnp.int32),
            pltpu.VMEM((table_rows, LANES), jnp.int32),
            pltpu.SMEM((table_rows, LANES), jnp.int32),
            pltpu.VMEM((owners, rows, depth), bf16),
            pltpu.VMEM((owners - 1, rows, depth), bf16),
            pltpu.VMEM((depth, everyone), bf16),
            pltpu.VMEM((2, rows, width), jnp.float32),
            pltpu.VMEM((owners - 1, 2, rows, width), bf16),
            pltpu.VMEM((owners - 1, 2, rows, width), bf16),
            pltpu.VMEM((2, everyone, width), bf16),
            pltpu.VMEM((rows, width), bf16),
            dma((2,)),
            dma((2,)),
            dma((2,)),
            dma,
            dma,
            dma((2, line, parts)),
            dma((line, parts)),
            dma((line, parts)),
            dma((owners - 1, panels, parts)),
            dma((owners, panels, parts)),
            dma((owners, panels, parts)),
            dma((owners - 1, halves + 1, chunks)),
            dma((owners - 1, halves + 1, chunks)),
            dma((owners - 1, 2, chunks)),
            dma((owners - 1, 2, chunks)),
        ],
        compiler_params=pltpu.CompilerParams(
            collective_id=0, has_side_effects=True, vmem_limit_bytes=28 << 20
        ),
        cost_estimate=pl.CostEstimate(
            flops=4 * everyone * depth * width,
            bytes_accessed=4 * capacity * block**2,
            transcendentals=2 * rows * width,
        ),
    )(tokens, gate_blocks, up_blocks, *lists, *counts, cotangent)


def place_kernel(table, terms_gate, terms_up, kept, hidden, gate_grad, up_grad, sems, hidden_sem):
    capacity = gate_grad.shape[0]
    positions = terms_gate.shape[0] - 1
    groups = up_to(capacity, LANES) // LANES
    base = 2 * up_to(positions, LANES) // LANES
    hidden_copy = pltpu.make_async_copy(kept, hidden, hidden_sem)
    hidden_copy.start()
    pairs = ((terms_gate, gate_grad), (terms_up, up_grad))
    for m, (terms, out) in enumerate(pairs):
        for g in range(groups):

            @pl.loop(0, min(LANES, capacity - g * LANES), unroll=8)
            def _(j):
                source = terms.at[table[base + m * groups + g, j]]
                pltpu.make_async_copy(source, out.at[g * LANES + j], sems.at[m]).start()

    for m, (_, out) in enumerate(pairs):
        pltpu.make_async_copy(out, out, sems.at[m]).wait()
    hidden_copy.wait()


def place(table, terms_gate, terms_up, hidden, capacity):
    shape = jax.ShapeDtypeStruct((capacity, *terms_gate.shape[1:]), jnp.bfloat16)
    hbm = pl.BlockSpec(memory_space=pl.ANY)
    vmem = pl.BlockSpec(memory_space=pltpu.VMEM)
    return pl.pallas_call(
        place_kernel,
        out_shape=(jax.ShapeDtypeStruct(hidden.shape, hidden.dtype), shape, shape),
        in_specs=[pl.BlockSpec(memory_space=pltpu.SMEM), vmem, vmem, vmem],
        out_specs=(hbm,) * 3,
        scratch_shapes=[pltpu.SemaphoreType.DMA((2,)), pltpu.SemaphoreType.DMA],
        compiler_params=pltpu.CompilerParams(vmem_limit_bytes=28 << 20),
        cost_estimate=pl.CostEstimate(
            flops=0, bytes_accessed=4 * capacity * terms_gate.shape[1] ** 2, transcendentals=0
        ),
    )(
        table,
        pltpu.with_memory_space_constraint(terms_gate, pltpu.VMEM),
        pltpu.with_memory_space_constraint(terms_up, pltpu.VMEM),
        pltpu.with_memory_space_constraint(hidden, pltpu.VMEM),
    )


def shards(tokens, gate_blocks, up_blocks, gate_list, gate_count, up_list, up_count, cotangent):
    owners = lax.axis_size("token")
    capacity, block = gate_blocks.shape[2:4]
    short = up_to(capacity, LANES) - capacity
    lists = [gate_list, up_list]
    if short:
        lists = [jnp.pad(x, ((0, 0), (0, 0), (0, short)), constant_values=-1) for x in lists]
    counts = [gate_count.reshape(owners), up_count.reshape(owners)]
    hidden, terms_gate, terms_up, table = exchange(
        tokens, gate_blocks[0, 0], up_blocks[0, 0], lists, counts, cotangent,
        owners, lax.axis_size("weight"), lax.axis_size("sub"),
    )
    hidden, gate_grad, up_grad = place(table, terms_gate, terms_up, hidden, capacity)
    shape = (1, 1, capacity, block, block)
    return (hidden, gate_grad.reshape(shape), up_grad.reshape(shape))


def solution(mesh):
    return jax.shard_map(
        shards,
        mesh=mesh,
        in_specs=(
            P(("groups", "token"), ("weight", "sub")),
            P("token", ("weight", "sub"), None, None, None),
            P("token", ("weight", "sub"), None, None, None),
            P(None, ("weight", "sub"), None),
            P(None, ("weight", "sub")),
            P(None, ("weight", "sub"), None),
            P(None, ("weight", "sub")),
            P(("groups", "token"), ("weight", "sub")),
        ),
        out_specs=(
            P(("groups", "token"), ("weight", "sub")),
            P(("groups", "token"), ("weight", "sub"), None, None, None),
            P(("groups", "token"), ("weight", "sub"), None, None, None),
        ),
        check_vma=False,
    )
```

```python
import jax
import jax.numpy as jnp
from jax import lax
from jax.experimental import pallas as pl
from jax.experimental.pallas import tpu as pltpu
from jax.sharding import PartitionSpec as P

MESH = pl.DeviceIdType.MESH
LANES = 128


def up_to(size, step):
    return -(-size // step) * step


def fill_table(table, lists, counts, me, positions):
    n = up_to(positions, LANES) // LANES
    groups = lists.shape[3] // LANES
    table[...] = jnp.zeros(table.shape, jnp.int32)
    slot = lax.broadcasted_iota(jnp.int32, (LANES, LANES), 0)
    lane = lax.broadcasted_iota(jnp.int32, (LANES, LANES), 1)
    for m in range(2):
        count = counts[m][me]
        found = [jnp.full((1, LANES), positions, jnp.int32) for _ in range(n)]
        for g in range(groups):
            row = lists[m, me, :, g * LANES : (g + 1) * LANES]
            column = jnp.broadcast_to(row, (LANES, LANES)).T
            column = jnp.where(slot + g * LANES < count, column, -1)
            for i in range(n):
                hit = jnp.where(column == lane + i * LANES, slot + g * LANES, positions)
                found[i] = jnp.minimum(found[i], jnp.min(hit, axis=0, keepdims=True))
            at = 2 * n + m * groups + g
            live = lane[0:1] + g * LANES < count
            table[at : at + 1, :] = jnp.where(live, row, positions)
        for i in range(n):
            table[m * n + i : m * n + i + 1, :] = found[i]


def exchange_kernel(
    tokens, gate_blocks, up_blocks, gate_list, up_list, gate_count, up_count, cotangent,
    hidden, terms_gate, terms_up, table,
    lists, slots, slots_s, own_x, other_x, flipped, own, sent, landed, delta_all, cot_all,
    block_sems, list_sems, table_sems, cot_sem, mine_sem,
    z_send, z_recv, x_send, x_recv, s_send, s_recv, p_send, p_recv, d_send, d_recv,
):
    held = (terms_gate, terms_up)
    owners = lax.axis_size("token")
    line = lax.axis_size("weight")
    subs = lax.axis_size("sub")
    me = lax.axis_index("token")
    here = lax.axis_index("weight")
    sub = lax.axis_index("sub")
    capacity, block, _ = gate_blocks.shape
    rows, local = tokens.shape
    depth = own_x.shape[2]
    width = hidden.shape[1]
    cols = width // block
    panels = line // owners
    parts = z_recv.shape[1]
    part = rows // parts
    chunks = p_send.shape[2]
    halves = p_send.shape[1] - 1
    piece = width // chunks
    tile = min(piece, 256)
    positions = depth * width // block**2
    tables = up_to(positions, LANES) // LANES
    sibling = {"sub": 1 - sub}
    ahead = [{"token": lax.rem(me + d, owners)} for d in range(owners)]
    behind = [{"token": lax.rem(me + owners - d, owners)} for d in range(owners)]
    left, right = {"weight": here - 1}, {"weight": here + 1}
    inner = here > 0
    outer = here < line - 1

    barrier = pltpu.get_barrier_semaphore()

    @pl.when(inner)
    def _():
        pl.semaphore_signal(barrier, inc=1, device_id=left, device_id_type=MESH)

    @pl.when(outer)
    def _():
        pl.semaphore_signal(barrier, inc=1, device_id=right, device_id_type=MESH)

    for d in range(1, owners):
        pl.semaphore_signal(barrier, inc=1, device_id=ahead[d], device_id_type=MESH)
    pl.semaphore_signal(barrier, inc=1, device_id=sibling, device_id_type=MESH)

    def span(q):
        return pl.ds(pl.multiple_of(q * part, part), part)

    def panel(o):
        return pl.ds(pl.multiple_of((lax.rem(o, panels) * subs + sub) * local, local), local)

    def own_at(o, q):
        return own_x.at[lax.div(o, panels), span(q), panel(o)]

    mine = pltpu.make_async_copy(tokens, own_x.at[lax.div(here, panels), :, panel(here)], mine_sem)
    list_copies = [
        pltpu.make_async_copy(source, lists.at[m], list_sems.at[m])
        for m, source in enumerate((gate_list, up_list))
    ]
    block_copies = [
        pltpu.make_async_copy(source, held[m].at[pl.ds(0, capacity)], block_sems.at[m])
        for m, source in enumerate((gate_blocks, up_blocks))
    ]
    cot_copy = pltpu.make_async_copy(cotangent, cot_all, cot_sem)
    mine.start()
    for copy in list_copies:
        copy.start()

    def z_copy(source, o, q, side):
        return pltpu.make_async_remote_copy(
            src_ref=source, dst_ref=own_at(o, q), send_sem=z_send.at[side, o, q], recv_sem=z_recv.at[o, q],
            device_id=(left, right)[side], device_id_type=MESH,
        )

    def cross_copy(source, o, q):
        half = lax.div(o, panels)
        d = lax.rem(half + owners - me, owners)
        return pltpu.make_async_remote_copy(
            src_ref=source, dst_ref=other_x.at[d - 1, span(q), panel(o)],
            send_sem=x_send.at[o, q], recv_sem=x_recv.at[d - 1, lax.rem(o, panels), q],
            device_id={"token": half}, device_id_type=MESH,
        )

    def sibling_copy(source, target, d, o, q):
        j = lax.rem(o, panels)
        return pltpu.make_async_remote_copy(
            src_ref=source, dst_ref=target, send_sem=s_send.at[d, j, q], recv_sem=s_recv.at[d, j, q],
            device_id=sibling, device_id_type=MESH,
        )

    def hand_on(source, o, q):
        @pl.when(lax.div(o, panels) == me)
        def _():
            sibling_copy(source, own_at(o, q), 0, o, q).start()

        @pl.when(lax.div(o, panels) != me)
        def _():
            cross_copy(source, o, q).start()

    pl.semaphore_wait(
        barrier, owners + inner.astype(jnp.int32) + outer.astype(jnp.int32)
    )
    def send_mine(q, side):
        @pl.when((inner, outer)[side])
        def _():
            z_copy(tokens.at[q * part : (q + 1) * part, :], here, q, side).start()

    at_home = lax.div(here, panels) == me
    gives_way = (at_home & (me < owners - 1), at_home & (me > 0))
    first = parts // 2 if line <= 4 else parts
    for q in range(parts):
        for side in range(2):
            if q < first:
                send_mine(q, side)
            else:

                @pl.when(jnp.logical_not(gives_way[side]))
                def _():
                    send_mine(q, side)

        hand_on(tokens.at[q * part : (q + 1) * part, :], here, q)
    for copy in block_copies:
        copy.start()
    cot_copy.start()

    zero = jnp.zeros((block, block), terms_gate.dtype)
    for m in range(2):
        held[m][positions] = zero
    for copy in list_copies:
        copy.wait()
    fill_table(slots, lists, (gate_count, up_count), me, positions)
    table_copies = [
        pltpu.make_async_copy(slots, slots_s, table_sems.at[0]),
        pltpu.make_async_copy(slots, table, table_sems.at[1]),
    ]
    for copy in table_copies:
        copy.start()

    def take_over(k, pieces):
        for d in range(1, owners):

            @pl.loop(0, panels)
            def _(j):
                o = me * panels + j

                @pl.when(lax.abs(o - here) == k)
                def _():
                    for q in pieces:
                        there = other_x.at[d - 1, span(q), panel(o)]
                        pltpu.make_async_remote_copy(
                            src_ref=there, dst_ref=there, send_sem=s_send.at[d, j, q],
                            recv_sem=x_recv.at[d - 1, j, q], device_id=sibling, device_id_type=MESH,
                        ).wait_recv()
                        sibling_copy(there, there, d, o, q).start()

    @pl.loop(1, line)
    def _(k):
        for side in range(2):
            o = here + k if side == 0 else here - k

            goes_on = (inner, outer)[side]

            @pl.when((o >= 0) & (o < line) & (goes_on | (lax.div(o, panels) != me)))
            def _():
                for q in range(parts):
                    z_copy(own_at(o, q), o, q, side).wait_recv()

                    @pl.when(goes_on)
                    def _():
                        z_copy(own_at(o, q), o, q, side).start()

                    hand_on(own_at(o, q), o, q)

            @pl.when(gives_way[side] & (k == (line - 1 - here if side == 0 else here)))
            def _():
                for q in range(first, parts):
                    send_mine(q, side)

        take_over(k - 1, range(parts))

    def take_late():
        @pl.loop(0, panels)
        def _(j):
            o = me * panels + j

            @pl.when((jnp.logical_not(inner) & (o > here)) | (jnp.logical_not(outer) & (o < here)))
            def _():
                for q in range(parts):
                    z_copy(own_at(o, q), o, q, 0).wait_recv()
                    sibling_copy(own_at(o, q), own_at(o, q), 0, o, q).start()

    def sibling_wait(d, recv, pieces):
        @pl.loop(0, panels)
        def _(j):
            o = me * panels + j
            for q in pieces:
                there = own_at(o, q) if d == 0 else other_x.at[d - 1, span(q), panel(o)]
                copy = sibling_copy(there, there, d, o, q)
                if recv:
                    copy.wait_recv()
                else:
                    copy.wait_send()

    def part_copy(d, m, h, c):
        size = rows // halves if m == 0 else rows
        across = pl.ds(h * size, size)
        at = pl.ds(pl.multiple_of(c * piece, piece), piece)
        return pltpu.make_async_remote_copy(
            src_ref=sent.at[d - 1, m, across, at], dst_ref=landed.at[d - 1, m, across, at],
            send_sem=p_send.at[d - 1, m * halves + h, c], recv_sem=p_recv.at[d - 1, m * halves + h, c],
            device_id=behind[d], device_id_type=MESH,
        )

    def delta_copy(d, m, c):
        at = pl.ds(pl.multiple_of(c * piece, piece), piece)
        return pltpu.make_async_remote_copy(
            src_ref=delta_all.at[m, pl.ds(0, rows), at], dst_ref=delta_all.at[m, pl.ds(d * rows, rows), at],
            send_sem=d_send.at[d - 1, m, c], recv_sem=d_recv.at[d - 1, m, c],
            device_id=ahead[d], device_id_type=MESH,
        )

    def product(x, m, first):
        strips = []
        for r in range(depth // block):
            line_of = []
            for q in range(tile // block):
                at = first + q + (r * cols) % LANES
                line_of.append(held[m][slots_s[m * tables + (r * cols) // LANES, at]])
            strips.append(jnp.concatenate(line_of, axis=1))
        return jnp.dot(x, jnp.concatenate(strips, axis=0), preferred_element_type=jnp.float32)

    def pass_on(m, h, size):
        for d in range(1, owners):

            @pl.loop(0, chunks)
            def _(c):
                for i in range(piece // tile):
                    at = pl.ds(pl.multiple_of(c * piece + i * tile, tile), tile)
                    first = c * (piece // block) + i * (tile // block)
                    value = product(other_x[d - 1, h * size : (h + 1) * size, :], m, first)
                    sent[d - 1, m, h * size : (h + 1) * size, at] = value.astype(sent.dtype)
                part_copy(d, m, h, c).start()

    def keep(m):
        @pl.loop(0, width // tile)
        def _(c):
            at = pl.ds(pl.multiple_of(c * tile, tile), tile)
            own[m, :, at] = product(own_x[me], m, c * (tile // block))

    def total(m, c):
        for d in range(1, owners):
            for h in range(halves if m == 0 else 1):
                part_copy(d, m, h, c).wait_recv()
        at = pl.ds(pl.multiple_of(c * piece, piece), piece)
        value = own[m, :, at]
        for d in range(1, owners):
            value = value + landed[d - 1, m, :, at].astype(jnp.float32)
        return value

    table_copies[0].wait()
    block_copies[0].wait()
    for h in range(halves):
        pieces = range(h * parts // halves, (h + 1) * parts // halves)
        take_over(line - 1, pieces)
        for d in range(1, owners):
            sibling_wait(d, True, pieces)
        pass_on(0, h, rows // halves)
    block_copies[1].wait()
    pass_on(1, 0, rows)
    mine.wait()
    take_late()
    sibling_wait(0, True, range(parts))
    keep(0)
    cot_copy.wait()

    @pl.loop(0, chunks)
    def _(c):
        at = pl.ds(pl.multiple_of(c * piece, piece), piece)
        gate = total(0, c)
        own[0, :, at] = gate
        silu = gate * jax.nn.sigmoid(gate)
        delta_all[1, 0:rows, at] = (cot_all[:, at].astype(jnp.float32) * silu).astype(delta_all.dtype)
        for d in range(1, owners):
            delta_copy(d, 1, c).start()

    keep(1)

    flip = min(depth, 256)
    for d in range(owners):

        @pl.loop(0, depth // flip)
        def _(i):
            at = pl.ds(pl.multiple_of(i * flip, flip), flip)
            value = own_x[me, :, at] if d == 0 else other_x[d - 1, :, at]
            flipped[at, d * rows : (d + 1) * rows] = value.T

    @pl.loop(0, chunks)
    def _(c):
        at = pl.ds(pl.multiple_of(c * piece, piece), piece)
        up = total(1, c)
        gate = own[0, :, at]
        sigmoid = jax.nn.sigmoid(gate)
        hidden[:, at] = (gate * sigmoid * up).astype(hidden.dtype)
        slope = sigmoid * (1.0 + gate * (1.0 - sigmoid))
        value = cot_all[:, at].astype(jnp.float32) * up * slope
        delta_all[0, 0:rows, at] = value.astype(delta_all.dtype)
        for d in range(1, owners):
            delta_copy(d, 0, c).start()

    for q in range(parts):

        @pl.loop(0, line)
        def _(o):
            @pl.when(inner & (o >= here))
            def _():
                z_copy(own_at(o, q), o, q, 0).wait_send()

            @pl.when(outer & (o <= here))
            def _():
                z_copy(own_at(o, q), o, q, 1).wait_send()

            @pl.when(lax.div(o, panels) != me)
            def _():
                cross_copy(own_at(o, q), o, q).wait_send()

    for d in range(owners):
        sibling_wait(d, False, range(parts))
    table_copies[1].wait()

    for m in (1, 0):

        @pl.loop(0, chunks)
        def _(c):
            for d in range(1, owners):
                delta_copy(d, m, c).wait_recv()
            at = pl.ds(pl.multiple_of(c * piece, piece), piece)
            term = jnp.dot(
                flipped[...], delta_all[m, :, at], preferred_element_type=jnp.float32
            ).astype(terms_gate.dtype)
            for r in range(depth // block):
                for q in range(piece // block):
                    p = r * cols + c * (piece // block) + q
                    held[m][p] = term[r * block : (r + 1) * block, q * block : (q + 1) * block]
            for d in range(1, owners):
                for h in range(halves if m == 0 else 1):
                    part_copy(d, m, h, c).wait_send()
                delta_copy(d, m, c).wait_send()


def exchange(tokens, gate_blocks, up_blocks, lists, counts, cotangent, owners, line, subs):
    rows, local = tokens.shape
    capacity, block, _ = gate_blocks.shape
    width = cotangent.shape[1]
    depth = local * line * subs // owners
    piece = min(width, 256)
    chunks = width // piece
    panels = line // owners
    parts = 4 if rows % 64 == 0 else 1
    halves = 2 if parts > 1 else 1
    everyone = owners * rows
    positions = depth * width // block**2
    table_rows = up_to(2 * up_to(positions, LANES) // LANES + 2 * lists[0].shape[2] // LANES, 8)
    blocks = pltpu.VMEM((positions + 1, block, block), jnp.bfloat16)
    dma = pltpu.SemaphoreType.DMA
    hbm = pl.BlockSpec(memory_space=pl.ANY)
    smem = pl.BlockSpec(memory_space=pltpu.SMEM)
    vmem = pl.BlockSpec(memory_space=pltpu.VMEM)
    bf16 = jnp.bfloat16
    return pl.pallas_call(
        exchange_kernel,
        out_shape=(
            pltpu.VMEM((rows, width), bf16),
            blocks,
            blocks,
            jax.ShapeDtypeStruct((table_rows, LANES), jnp.int32),
        ),
        in_specs=[hbm] * 5 + [smem] * 2 + [hbm],
        out_specs=(vmem, vmem, vmem, hbm),
        scratch_shapes=[
            pltpu.VMEM((2, *lists[0].shape), jnp.int32),
            pltpu.VMEM((table_rows, LANES), jnp.int32),
            pltpu.SMEM((table_rows, LANES), jnp.int32),
            pltpu.VMEM((owners, rows, depth), bf16),
            pltpu.VMEM((owners - 1, rows, depth), bf16),
            pltpu.VMEM((depth, everyone), bf16),
            pltpu.VMEM((2, rows, width), jnp.float32),
            pltpu.VMEM((owners - 1, 2, rows, width), bf16),
            pltpu.VMEM((owners - 1, 2, rows, width), bf16),
            pltpu.VMEM((2, everyone, width), bf16),
            pltpu.VMEM((rows, width), bf16),
            dma((2,)),
            dma((2,)),
            dma((2,)),
            dma,
            dma,
            dma((2, line, parts)),
            dma((line, parts)),
            dma((line, parts)),
            dma((owners - 1, panels, parts)),
            dma((owners, panels, parts)),
            dma((owners, panels, parts)),
            dma((owners - 1, halves + 1, chunks)),
            dma((owners - 1, halves + 1, chunks)),
            dma((owners - 1, 2, chunks)),
            dma((owners - 1, 2, chunks)),
        ],
        compiler_params=pltpu.CompilerParams(
            collective_id=0, has_side_effects=True, vmem_limit_bytes=28 << 20
        ),
        cost_estimate=pl.CostEstimate(
            flops=4 * everyone * depth * width,
            bytes_accessed=4 * capacity * block**2,
            transcendentals=2 * rows * width,
        ),
    )(tokens, gate_blocks, up_blocks, *lists, *counts, cotangent)


def place_kernel(table, terms_gate, terms_up, kept, hidden, gate_grad, up_grad, sems, hidden_sem):
    capacity = gate_grad.shape[0]
    positions = terms_gate.shape[0] - 1
    groups = up_to(capacity, LANES) // LANES
    base = 2 * up_to(positions, LANES) // LANES
    hidden_copy = pltpu.make_async_copy(kept, hidden, hidden_sem)
    hidden_copy.start()
    pairs = ((terms_gate, gate_grad), (terms_up, up_grad))
    for m, (terms, out) in enumerate(pairs):
        for g in range(groups):

            @pl.loop(0, min(LANES, capacity - g * LANES), unroll=8)
            def _(j):
                source = terms.at[table[base + m * groups + g, j]]
                pltpu.make_async_copy(source, out.at[g * LANES + j], sems.at[m]).start()

    for m, (_, out) in enumerate(pairs):
        pltpu.make_async_copy(out, out, sems.at[m]).wait()
    hidden_copy.wait()


def place(table, terms_gate, terms_up, hidden, capacity):
    shape = jax.ShapeDtypeStruct((capacity, *terms_gate.shape[1:]), jnp.bfloat16)
    hbm = pl.BlockSpec(memory_space=pl.ANY)
    vmem = pl.BlockSpec(memory_space=pltpu.VMEM)
    return pl.pallas_call(
        place_kernel,
        out_shape=(jax.ShapeDtypeStruct(hidden.shape, hidden.dtype), shape, shape),
        in_specs=[pl.BlockSpec(memory_space=pltpu.SMEM), vmem, vmem, vmem],
        out_specs=(hbm,) * 3,
        scratch_shapes=[pltpu.SemaphoreType.DMA((2,)), pltpu.SemaphoreType.DMA],
        compiler_params=pltpu.CompilerParams(vmem_limit_bytes=28 << 20),
        cost_estimate=pl.CostEstimate(
            flops=0, bytes_accessed=4 * capacity * terms_gate.shape[1] ** 2, transcendentals=0
        ),
    )(
        table,
        pltpu.with_memory_space_constraint(terms_gate, pltpu.VMEM),
        pltpu.with_memory_space_constraint(terms_up, pltpu.VMEM),
        pltpu.with_memory_space_constraint(hidden, pltpu.VMEM),
    )


def shards(tokens, gate_blocks, up_blocks, gate_list, gate_count, up_list, up_count, cotangent):
    owners = lax.axis_size("token")
    capacity, block = gate_blocks.shape[2:4]
    short = up_to(capacity, LANES) - capacity
    lists = [gate_list, up_list]
    if short:
        lists = [jnp.pad(x, ((0, 0), (0, 0), (0, short)), constant_values=-1) for x in lists]
    counts = [gate_count.reshape(owners), up_count.reshape(owners)]
    hidden, terms_gate, terms_up, table = exchange(
        tokens, gate_blocks[0, 0], up_blocks[0, 0], lists, counts, cotangent,
        owners, lax.axis_size("weight"), lax.axis_size("sub"),
    )
    hidden, gate_grad, up_grad = place(table, terms_gate, terms_up, hidden, capacity)
    shape = (1, 1, capacity, block, block)
    return (hidden, gate_grad.reshape(shape), up_grad.reshape(shape))


def solution(mesh):
    return jax.shard_map(
        shards,
        mesh=mesh,
        in_specs=(
            P(("groups", "token"), ("weight", "sub")),
            P("token", ("weight", "sub"), None, None, None),
            P("token", ("weight", "sub"), None, None, None),
            P(None, ("weight", "sub"), None),
            P(None, ("weight", "sub")),
            P(None, ("weight", "sub"), None),
            P(None, ("weight", "sub")),
            P(("groups", "token"), ("weight", "sub")),
        ),
        out_specs=(
            P(("groups", "token"), ("weight", "sub")),
            P(("groups", "token"), ("weight", "sub"), None, None, None),
            P(("groups", "token"), ("weight", "sub"), None, None, None),
        ),
        check_vma=False,
    )
```
